32 devices in a mesh: rel: 4 (over y, x), node: 4 (over z), feat: 2 (over core).
Axes of the slice: x: 2, y: 2, z: 4, core: 2. Of those that a mesh axis runs over, the one named last changes fastest.
Arguments:
- features: float32 [3072, 768], P('node', 'feat'), may hold values from -6 to 6
- tile_values: float32 [4, 12, 12, 256, 256], P('rel', 'node'), may hold values from -0.4375 to 0.4375
- tile_cols: int32 [4, 12, 12], P('rel', 'node'), may hold values from 0 to 11, as said below
- tile_count: int32 [4, 12], P('rel', 'node'), may hold values from 1 to 12, as said below
- degree: int32 [4, 3072], P('rel', 'node'), may hold values from 1 to 16
- proj_weight: float32 [4, 768, 512], P('rel', 'feat'), may hold values from -0.21875 to 0.21875
- proj_bias: float32 [4, 512], P('rel', 'feat'), may hold values from -3 to 3
Outputs:
- metapath_out: float32 [4, 3072, 512], P(None, ('node', 'rel'), 'feat')
The draws below stay inside these ranges and needn't reach their ends.
Inputs may be any that keep to these rules, and one draw needn't show every extreme that they name: `tile_cols`: within one row of tiles the 12 column tiles are distinct; slots at or past the count hold valid tile numbers that are not used. `tile_count`: in every relation some row of tiles has exactly 12 live slots.
All inputs are finite; a program needn't handle non-finite values.
Results may differ from the reference program's by a relative error of at most 0.0001.
Values sent between devices are 32-bit elements; how exact they have to be, the bound alone decides.
A program may use at most 128 MiB of HBM per device.

```python
import jax
import jax.numpy as jnp
from jax import lax

F = 768
HID = 512
TILE = 256
K = 12
REL = 4
NODES = 3072
NTILES = 12


def draw_tile_cols(key, part):
    row_keys = jax.random.split(key, REL * NTILES)

    def choose(one_key):
        return jax.random.permutation(one_key, NTILES)[:K]
    picked = jax.vmap(choose)(row_keys)
    return picked.reshape(REL, NTILES, K).astype(jnp.int32)


def draw_tile_count(key, part):
    drawn = jax.random.randint(key, (REL, NTILES), 1, K + 1)
    full_row = jax.random.randint(jax.random.fold_in(key, 7), (REL,), 0, NTILES)
    is_full = jnp.arange(NTILES)[None, :] == full_row[:, None]
    return jnp.where(is_full, K, drawn).astype(jnp.int32)


def place_ends(array, stream_key, smallest, high):
    longest = array.shape.index(max(array.shape))
    spots = []
    for shift in (0, 1):
        where = [jax.random.randint(jax.random.fold_in(stream_key, axis), (), 0, length) for axis, length in enumerate(array.shape)]
        where[longest] = (where[longest] + shift) % array.shape[longest]
        spots.append(tuple(where))
    return array.at[spots[0]].set(smallest).at[spots[1]].set(high)


def block_levels(own_key, dims, cuts, smallest, top_value):
    def one(axis_at, shards_of):
        draws = jax.random.uniform(jax.random.fold_in(jax.random.fold_in(own_key, 6), axis_at), (shards_of,), jnp.float32, smallest / len(cuts), top_value / len(cuts))
        return jnp.repeat(jnp.exp(draws), dims[axis_at] // shards_of).reshape((-1,) + (1,) * (len(dims) - axis_at - 1))

    level = one(*cuts[0])
    for cut in cuts[1:]:
        level = level * one(*cut)
    return level


def noise(stream_key, shape, width, bound, shards=(), held_as=jnp.bfloat16):
    factor_of = block_levels(stream_key, shape, shards, -0.22, 0.18) if shards else 1.0
    values = jax.random.normal(stream_key, shape, jnp.float32) * width * factor_of
    return jnp.minimum(jnp.maximum(values, -bound), bound).astype(held_as)


def setup_inputs(seed: int = 0) -> dict:
    arg_keys = jax.random.split(jax.random.key(seed), 8)
    return {
        "features": noise(arg_keys[0], (NODES, F), 1.0, 6.0, ((0, 4), (1, 2)), jnp.float32),
        "tile_values": noise(arg_keys[1], (REL, NTILES, K, TILE, TILE), (TILE * K // 16) ** -0.5, 0.4375, ((0, 4), (1, 4)), jnp.float32),
        "tile_cols": draw_tile_cols(jax.random.fold_in(arg_keys[7], 71), 0),
        "tile_count": draw_tile_count(jax.random.fold_in(arg_keys[7], 71), 0),
        "degree": place_ends(jax.random.randint(arg_keys[4], (REL, NODES), 1, 17), jax.random.fold_in(arg_keys[4], 1), 1, 16).astype(jnp.int32),
        "proj_weight": noise(arg_keys[5], (REL, F, HID), F ** -0.5, 0.21875, ((0, 4), (1, 2)), jnp.float32),
        "proj_bias": noise(arg_keys[6], (REL, HID), 0.5, 3.0, ((0, 4), (1, 2)), jnp.float32),
    }


def one_hop(current, values, cols, count, row_scale):
    columns = current.shape[1]
    tile_rows = (row_scale[:, None] * current).reshape(NTILES, TILE, columns)
    live_mask = (jnp.arange(K)[None, :] < count[:, None]).astype(current.dtype)

    def row_tile(items):
        values_row, cols_row, mask_row = items
        sources = tile_rows[cols_row]
        kept = values_row * mask_row[:, None, None]
        return jnp.einsum('kab,kbw->aw', kept, sources, precision=lax.Precision.HIGHEST)
    summed = lax.map(row_tile, (values, cols, live_mask))
    return row_scale[:, None] * summed.reshape(NODES, columns)

def reference(features, tile_values, tile_cols, tile_count, degree, proj_weight, proj_bias):
    results = []
    for relation in range(REL):
        row_scale = lax.rsqrt(degree[relation].astype(jnp.float32))
        first = one_hop(features, tile_values[relation], tile_cols[relation], tile_count[relation], row_scale)
        second = one_hop(first, tile_values[relation], tile_cols[relation], tile_count[relation], row_scale)
        projected = jnp.dot(second, proj_weight[relation], precision=lax.Precision.HIGHEST, preferred_element_type=jnp.float32)
        results.append(projected + proj_bias[relation][None, :])
    return jnp.stack(results)
```

```python
import functools

import jax
import jax.numpy as jnp
from jax import lax
from jax.experimental import pallas as pl
from jax.experimental.pallas import tpu as pltpu
from jax.sharding import PartitionSpec as P

MESH = pl.DeviceIdType.MESH
LANES = 128
SUBLANES = 8
Z_INDEX = {("F", 0): 3, ("F", 1): 4, ("F", 2): 5, ("X", 0): 6, ("Y", 0): 7, ("Y", 1): 8}


def split(x):
    high = x.astype(jnp.bfloat16)
    return high, (x - high.astype(jnp.float32)).astype(jnp.bfloat16)


def dot(a, b):
    return jnp.dot(a, b, preferred_element_type=jnp.float32)


def product(a_high, a_low, b_high, b_pair):
    width = b_high.shape[1]
    both = dot(a_high, b_pair)
    return both[:, :width] + both[:, width:] + dot(a_low, b_high)


def both_and(*terms):
    return functools.reduce(jnp.logical_and, terms)


def kernel(
    sizes,
    tile_cols,
    tile_count,
    degree,
    weight,
    bias,
    features_hbm,
    tiles_hbm,
    out,
    slot_of,
    scale,
    tiles,
    a_high,
    a_low,
    w_pair,
    raw,
    scales,
    first,
    field,
    total,
    partial_out,
    partial_in,
    load_sem,
    scale_send,
    scale_recv,
    raw_recv,
    z_send,
    x_send,
    y_send,
    pair_send,
    pair_recv,
    line_send,
    line_recv,
    out_send,
    out_recv,
):
    nodes, rels, chunks = sizes
    rows, depth = raw.shape[1:]
    row_tiles, slots, tile = tiles.shape[:3]
    width = chunks * LANES
    col_tiles = nodes * row_tiles
    group = rows // rels
    unit = tile // rels
    last = nodes - 1
    rel, node, feat = (lax.axis_index(name) for name in ("rel", "node", "feat"))
    has_up, has_down = node < last, node > 0
    x_rel, y_rel, far_rel = rel + 1 - 2 * lax.rem(rel, 2), lax.rem(rel + 2, rels), rels - 1 - rel
    owner = {"O": rel, "X": x_rel, "Y": y_rel, "F": far_rel}

    barrier = pltpu.get_barrier_semaphore()
    pl.semaphore_signal(barrier, inc=1, device_id={"feat": 1 - feat}, device_id_type=MESH)
    for step in range(1, rels):
        peer = lax.rem(rel + step, rels)
        pl.semaphore_signal(barrier, inc=1, device_id={"rel": peer}, device_id_type=MESH)
    for step in range(1, nodes):
        peer = lax.rem(node + step, nodes)
        pl.semaphore_signal(barrier, inc=1, device_id={"node": peer}, device_id_type=MESH)
    features_copy = pltpu.make_async_copy(features_hbm, raw.at[node], load_sem.at[0])
    features_copy.start()
    tiles_copy = pltpu.make_async_copy(tiles_hbm, tiles, load_sem.at[1])
    tiles_copy.start()
    row_scale = lax.rsqrt(degree[...].astype(jnp.float32))
    scales[node] = jnp.zeros(scales.shape[1:], jnp.float32)
    for t in range(row_tiles):
        scales[node, t : t + 1, :] = row_scale[:, t * tile : (t + 1) * tile]
    features_copy.wait()
    pl.semaphore_wait(barrier, rels + nodes - 1)

    def remote(src, dst, send_sem, recv_sem, **device):
        return pltpu.make_async_remote_copy(
            src_ref=src,
            dst_ref=dst,
            send_sem=send_sem,
            recv_sem=recv_sem,
            device_id=device,
            device_id_type=MESH,
        )

    def scale_copy(slot, step):
        peer = lax.rem(node + step, nodes)
        return remote(
            scales.at[slot], scales.at[slot], scale_send.at[step], scale_recv.at[slot], node=peer
        )

    def tile_rows(t):
        return pl.ds(pl.multiple_of(t * tile, tile), tile)

    def piece(slot, t, kind):
        start = pl.multiple_of(t * tile + owner[kind] * unit, unit)
        return raw.at[slot, pl.ds(start, unit), :], raw_recv.at[slot, t, owner[kind]]

    def z_copy(way, slot, kind, t):
        ref, recv_sem = piece(slot, t, kind)
        index = t if kind == "O" else Z_INDEX[kind, t]
        neighbour = node + 1 if way == 0 else node - 1
        return remote(ref, ref, z_send.at[way, slot, index], recv_sem, node=neighbour)

    def x_copy(slot, kind, t):
        ref, recv_sem = piece(slot, t, kind)
        index = t if kind == "O" else row_tiles
        return remote(ref, ref, x_send.at[slot, index], recv_sem, rel=x_rel)

    def y_copy(slot, kind, t):
        ref, recv_sem = piece(slot, t, kind)
        index = t if kind == "O" else row_tiles
        return remote(ref, ref, y_send.at[slot, index], recv_sem, rel=y_rel)

    def arrived(slot, kind, t):
        x_copy(slot, kind, t).wait_recv()

    def inner(i):
        return jnp.logical_and(i > 0, i < last)

    def is_end(i):
        return jnp.logical_or(i == 0, i == last)

    def plans(source, receiver, near):
        inside = jnp.logical_and(near, inner(receiver))
        rich = jnp.logical_and(inside, is_end(source))
        middle = jnp.logical_and(inside, inner(source))
        return rich, middle

    def exists(way, s):
        return node - s >= 0 if way == 0 else node + s < nodes

    def slot_at(way, s):
        return node - s if way == 0 else node + s

    def onward(way):
        return has_up if way == 0 else has_down

    def on_sides(s, act):
        for way in range(2):

            @pl.when(exists(way, s))
            def _(way=way):
                act(way, slot_at(way, s))

    def x_sends(slot, s):
        rich, middle = plans(slot, node, s == 1)
        plain = jnp.logical_not(jnp.logical_or(rich, middle))
        yield jnp.logical_not(rich), functools.partial(x_copy, slot, "O", 0)
        yield None, functools.partial(x_copy, slot, "O", 1)
        yield None, functools.partial(x_copy, slot, "O", 2)
        yield plain, functools.partial(x_copy, slot, "Y", 0)

    def y_sends(slot, s):
        rich, middle = plans(slot, node, s == 1)
        plain = jnp.logical_not(jnp.logical_or(rich, middle))
        yield jnp.logical_not(rich), functools.partial(y_copy, slot, "O", 0)
        yield jnp.logical_not(rich), functools.partial(y_copy, slot, "O", 1)
        yield None, functools.partial(y_copy, slot, "O", 2)
        yield plain, functools.partial(y_copy, slot, "X", 1)
        yield middle, functools.partial(y_copy, slot, "X", 0)

    def z_extras(way):
        neighbour = node + 1 if way == 0 else node - 1
        rich, middle = plans(node, neighbour, True)
        yield None, functools.partial(z_copy, way, node, "F", 2)
        yield rich, functools.partial(z_copy, way, node, "F", 0)
        yield rich, functools.partial(z_copy, way, node, "X", 0)
        yield rich, functools.partial(z_copy, way, node, "Y", 0)
        yield jnp.logical_or(rich, middle), functools.partial(z_copy, way, node, "F", 1)
        yield rich, functools.partial(z_copy, way, node, "Y", 1)

    def act_if(condition, act):
        if condition is None:
            act()
        else:
            pl.when(condition)(act)

    def take_own(s, t):
        def act(way, slot):
            arrived(slot, "O", t)

            @pl.when(onward(way))
            def _():
                z_copy(way, slot, "O", t).start()

            for sends in (x_sends, y_sends):
                condition, copy = list(sends(slot, s))[t]
                act_if(condition, lambda: copy().start())

        on_sides(s, act)

    def relay_x(way, slot, s):
        condition, copy = list(x_sends(slot, s))[3]

        @pl.when(condition)
        def _():
            arrived(slot, "Y", 0)
            copy().start()

    def relay_y(way, slot, s):
        _, _, _, (plain, from_one), (middle, from_zero) = y_sends(slot, s)

        @pl.when(plain)
        def _():
            arrived(slot, "X", 1)
            from_one().start()

        @pl.when(middle)
        def _():
            arrived(slot, "X", 0)
            from_zero().start()

    def relay_pending(s, relay):
        for way in range(2):

            @pl.when(both_and(exists(way, s), exists(way, s + 1)))
            def _(way=way):
                relay(way, slot_at(way, s), s)

    def relay_final(s):
        for way in range(2):

            @pl.when(both_and(exists(way, s), jnp.logical_not(exists(way, s + 1))))
            def _(way=way):
                relay_x(way, slot_at(way, s), s)
                relay_y(way, slot_at(way, s), s)

    def finish_raw(way, slot, s, t):
        rich, middle = plans(slot, node, s == 1)
        plain = jnp.logical_not(jnp.logical_or(rich, middle))
        if t == 2:
            arrived(slot, "F", 2)

            @pl.when(onward(way))
            def _():
                z_copy(way, slot, "F", 2).start()

            arrived(slot, "X", 2)
            arrived(slot, "Y", 2)
        elif t == 1:
            arrived(slot, "F", 1)
            arrived(slot, "Y", 1)
            act_if(jnp.logical_not(plain), lambda: arrived(slot, "X", 1))
        else:
            arrived(slot, "F", 0)
            act_if(jnp.logical_not(middle), lambda: arrived(slot, "X", 0))
            act_if(jnp.logical_not(plain), lambda: arrived(slot, "Y", 0))

    def add_products(acc, b_high, b_pair, column):
        for m in range(row_tiles):
            k = slot_of[m * col_tiles + column]
            acc[m * tile : (m + 1) * tile, :] += product(a_high[m, k], a_low[m, k], b_high, b_pair)

    def add_first(slot, t):
        b_high, b_low = split(raw[slot, tile_rows(t), :])
        add_products(first, b_high, jnp.concatenate([b_high, b_low], axis=1), slot * row_tiles + t)

    def prepare(t):
        def one(k, carry):
            c = tile_cols[0, t, k]
            live = (k < tile_count[0, t]).astype(jnp.float32)
            column_scale = scales[lax.div(c, row_tiles), pl.ds(lax.rem(c, row_tiles), 1), :]
            high, low = split(tiles[t, k] * (column_scale * live))
            a_high[t, k] = high
            a_low[t, k] = low
            return carry

        lax.fori_loop(0, slots, one, 0)
        a_high[t, slots] = jnp.zeros((tile, tile), jnp.bfloat16)
        a_low[t, slots] = jnp.zeros((tile, tile), jnp.bfloat16)

    for step in range(1, nodes):
        scale_copy(node, step).start()
    for t in range(row_tiles):
        for way in range(2):

            @pl.when(onward(way))
            def _(way=way, t=t):
                z_copy(way, node, "O", t).start()

    def send_extras():
        for way in range(2):

            @pl.when(onward(way))
            def _(way=way):
                for condition, copy in z_extras(way):
                    act_if(condition, lambda: copy().start())

    pl.when(is_end(node))(send_extras)
    for t in range(row_tiles):

        def find(c, carry, t=t):
            found = jnp.int32(slots)
            for k in range(slots):
                found = jnp.where(tile_cols[0, t, k] == c, k, found)
            slot_of[t * col_tiles + c] = found
            return carry

        lax.fori_loop(0, col_tiles, find, 0)
    w_high, w_low = split(weight[...])
    for side in range(2):
        w_pair[side, :, :width] = w_high[:, side * width : (side + 1) * width]
        w_pair[side, :, width:] = w_low[:, side * width : (side + 1) * width]
    for block in range(rows // LANES):
        lanes = slice(block * LANES, (block + 1) * LANES)
        scale[lanes, :] = jnp.broadcast_to(row_scale[:, lanes], (LANES, LANES)).T
    first[...] = jnp.zeros_like(first)
    total[...] = jnp.zeros_like(total)
    for step in range(1, nodes):
        scale_copy(lax.rem(node + step, nodes), 1).wait_recv()
    tiles_copy.wait()
    for t in range(row_tiles):
        prepare(t)
        take_own(1, t)
    pl.when(inner(node))(send_extras)
    if nodes <= 2:
        relay_final(1)

    def own_first(t, carry):
        add_first(node, t)
        return carry

    lax.fori_loop(0, row_tiles, own_first, 0)

    def use_raw(s):
        for t in (2, 0, 1):

            def act(way, slot, t=t):
                finish_raw(way, slot, s, t)
                add_first(slot, t)

            on_sides(s, act)

    def first_step(s, carry):
        @pl.when(s == 2)
        def _():
            for way in range(2):

                @pl.when(both_and(exists(way, 1), jnp.logical_not(exists(way, 2))))
                def _(way=way):
                    relay_x(way, slot_at(way, 1), 1)
                    relay_y(way, slot_at(way, 1), 1)

        take_own(s, 0)
        relay_pending(s - 1, relay_x)
        take_own(s, 1)
        relay_pending(s - 1, relay_y)
        take_own(s, 2)
        relay_final(s)
        use_raw(s - 1)
        return carry

    lax.fori_loop(2, nodes, first_step, 0)
    use_raw(last)

    def project(side, t):
        f_high, f_low = split(first[tile_rows(t), :])
        pair = w_pair[side]
        return product(f_high, f_low, pair[:, :width], pair)

    def pair_copy(t):
        return remote(
            partial_out.at[t], partial_in.at[t], pair_send.at[t], pair_recv.at[t], feat=1 - feat
        )

    def line_copy(chunk, way, slot, t):
        neighbour = node + 1 if way == 0 else node - 1
        ref = field.at[chunk, slot, tile_rows(t), :]
        return remote(
            ref,
            ref,
            line_send.at[chunk, way, slot, t],
            line_recv.at[chunk, slot, t],
            node=neighbour,
        )

    def add_field(chunk, slot, t):
        b_high, b_low = split(field[chunk, slot, tile_rows(t), :])
        column = slot * row_tiles + t
        add_products(total.at[chunk], b_high, jnp.concatenate([b_high, b_low], axis=1), column)

    def send_own(chunk, t):
        for way in range(2):

            @pl.when(onward(way))
            def _(way=way):
                line_copy(chunk, way, node, t).start()

    def take(chunk, s):
        def one(t, carry):
            def forward(way, slot):
                line_copy(chunk, way, slot, t).wait_recv()

                @pl.when(onward(way))
                def _():
                    line_copy(chunk, way, slot, t).start()

            on_sides(s, forward)
            on_sides(s, lambda way, slot: add_field(chunk, slot, t))
            return carry

        lax.fori_loop(0, row_tiles, one, 0)

    for t in range(row_tiles):
        partial_out[t] = project(1 - feat, t)
        pair_copy(t).start()
    for t in range(row_tiles):
        mine = project(feat, t)
        pair_copy(t).wait_recv()
        mine = mine + partial_in[t]
        for chunk in range(chunks):
            columns = slice(chunk * LANES, (chunk + 1) * LANES)
            row_slice = slice(t * tile, (t + 1) * tile)
            field[chunk, node, row_slice, :] = scale[row_slice, :] * mine[:, columns]
        send_own(0, t)

    def out_copy(chunk, step):
        peer = lax.rem(rel + step, rels)
        return remote(
            total.at[chunk, pl.ds(pl.multiple_of(peer * group, 8), group), :],
            out.at[rel, :, pl.ds(chunk * LANES, LANES)],
            out_send.at[chunk, step],
            out_recv.at[chunk, step],
            rel=peer,
        )

    def in_copy(chunk, step):
        peer = lax.rem(rel + rels - step, rels)
        return remote(
            total.at[chunk, pl.ds(0, group), :],
            out.at[peer, :, pl.ds(chunk * LANES, LANES)],
            out_send.at[chunk, step],
            out_recv.at[chunk, step],
            rel=peer,
        )

    def finish(chunk):
        columns = slice(chunk * LANES, (chunk + 1) * LANES)
        total[chunk] = scale[...] * total[chunk] + bias[:, columns]
        for step in range(1, rels):
            out_copy(chunk, step).start()
        own = pl.ds(pl.multiple_of(rel * group, 8), group)
        out[rel, :, columns] = total[chunk, own, :]

    def add_own(chunk):
        def one(t, carry):
            add_field(chunk, node, t)
            return carry

        lax.fori_loop(0, row_tiles, one, 0)

    add_own(0)
    take(0, 1)
    for chunk in range(1, chunks):
        for t in range(row_tiles):
            send_own(chunk, t)
        add_own(chunk)

    def hop_step(s, carry):
        take(0, s)
        for chunk in range(1, chunks):
            take(chunk, s - 1)
        return carry

    lax.fori_loop(2, nodes, hop_step, 0)
    finish(0)

    def drain_raw(slot, carry):
        for way in range(2):
            mine = slot <= node if way == 0 else slot >= node

            @pl.when(both_and(onward(way), mine))
            def _(way=way):
                for t in range(row_tiles):
                    z_copy(way, slot, "O", t).wait_send()

            @pl.when(both_and(onward(way), mine, slot != node))
            def _(way=way):
                z_copy(way, slot, "F", 2).wait_send()

        @pl.when(slot != node)
        def _():
            s = jnp.abs(slot - node)
            for sends in (x_sends, y_sends):
                for condition, copy in sends(slot, s):
                    act_if(condition, lambda: copy().wait_send())

        return carry

    lax.fori_loop(0, nodes, drain_raw, 0)
    for way in range(2):

        @pl.when(onward(way))
        def _(way=way):
            for condition, copy in z_extras(way):
                act_if(condition, lambda: copy().wait_send())

    for step in range(1, nodes):
        scale_copy(node, step).wait_send()
    for t in range(row_tiles):
        pair_copy(t).wait_send()
    for chunk in range(1, chunks):
        take(chunk, last)
        finish(chunk)

    def drain_line(slot, carry):
        for way in range(2):
            mine = slot <= node if way == 0 else slot >= node

            @pl.when(both_and(onward(way), mine))
            def _(way=way):
                for chunk in range(chunks):
                    for t in range(row_tiles):
                        line_copy(chunk, way, slot, t).wait_send()

        return carry

    lax.fori_loop(0, nodes, drain_line, 0)
    for chunk in range(chunks):
        for step in range(1, rels):
            out_copy(chunk, step).wait_send()
            in_copy(chunk, step).wait_recv()


def on_device(
    nodes, rels, features, tile_values, tile_cols, tile_count, degree, proj_weight, proj_bias
):
    rows, depth = features.shape
    _, row_tiles, slots, tile, _ = tile_values.shape
    width = proj_bias.shape[1]
    chunks = width // LANES
    col_tiles = nodes * row_tiles
    vmem = pl.BlockSpec(memory_space=pltpu.VMEM)
    smem = pl.BlockSpec(memory_space=pltpu.SMEM)
    dma = pltpu.SemaphoreType.DMA
    return pl.pallas_call(
        functools.partial(kernel, (nodes, rels, chunks)),
        out_shape=jax.ShapeDtypeStruct((rels, rows // rels, width), jnp.float32),
        in_specs=[smem, smem, vmem, vmem, vmem] + [pl.BlockSpec(memory_space=pl.ANY)] * 2,
        out_specs=vmem,
        scratch_shapes=[
            pltpu.SMEM((row_tiles * col_tiles,), jnp.int32),
            pltpu.VMEM((rows, LANES), jnp.float32),
            pltpu.VMEM((row_tiles, slots, tile, tile), jnp.float32),
            pltpu.VMEM((row_tiles, slots + 1, tile, tile), jnp.bfloat16),
            pltpu.VMEM((row_tiles, slots + 1, tile, tile), jnp.bfloat16),
            pltpu.VMEM((2, depth, 2 * width), jnp.bfloat16),
            pltpu.VMEM((nodes, rows, depth), jnp.float32),
            pltpu.VMEM((nodes, SUBLANES, tile), jnp.float32),
            pltpu.VMEM((rows, depth), jnp.float32),
            pltpu.VMEM((chunks, nodes, rows, LANES), jnp.float32),
            pltpu.VMEM((chunks, rows, LANES), jnp.float32),
            pltpu.VMEM((row_tiles, tile, width), jnp.float32),
            pltpu.VMEM((row_tiles, tile, width), jnp.float32),
            dma((2,)),
            dma((nodes,)),
            dma((nodes,)),
            dma((nodes, row_tiles, rels)),
            dma((2, nodes, 9)),
            dma((nodes, row_tiles + 1)),
            dma((nodes, row_tiles + 1)),
            dma((row_tiles,)),
            dma((row_tiles,)),
            dma((chunks, 2, nodes, row_tiles)),
            dma((chunks, nodes, row_tiles)),
            dma((chunks, rels)),
            dma((chunks, rels)),
        ],
        compiler_params=pltpu.CompilerParams(
            collective_id=0, has_side_effects=True, vmem_limit_bytes=60 << 20
        ),
    )(
        tile_cols,
        tile_count,
        degree,
        proj_weight[0],
        proj_bias,
        features,
        tile_values[0],
    )


def solution(mesh):
    return jax.shard_map(
        functools.partial(on_device, mesh.shape["node"], mesh.shape["rel"]),
        mesh=mesh,
        in_specs=(
            P("node", "feat"),
            P("rel", "node", None, None, None),
            P("rel", "node", None),
            P("rel", "node"),
            P("rel", "node"),
            P("rel", "feat", None),
            P("rel", "feat"),
        ),
        out_specs=P(None, ("node", "rel"), "feat"),
        check_vma=False,
    )
```

```python
import functools

import jax
import jax.numpy as jnp
from jax import lax
from jax.experimental import pallas as pl
from jax.experimental.pallas import tpu as pltpu
from jax.sharding import PartitionSpec as P

MESH = pl.DeviceIdType.MESH
LANES = 128
SUBLANES = 8
Z_INDEX = {("F", 0): 3, ("F", 1): 4, ("F", 2): 5, ("X", 0): 6, ("Y", 0): 7, ("X", 1): 8, ("Y", 1): 9}


def split(x):
    high = x.astype(jnp.bfloat16)
    return high, (x - high.astype(jnp.float32)).astype(jnp.bfloat16)


def dot(a, b):
    return jnp.dot(a, b, preferred_element_type=jnp.float32)


def product(a_high, a_low, b_high, b_pair):
    width = b_high.shape[1]
    both = dot(a_high, b_pair)
    return both[:, :width] + both[:, width:] + dot(a_low, b_high)


def both_and(*terms):
    return functools.reduce(jnp.logical_and, terms)


def kernel(
    sizes,
    tile_cols,
    tile_count,
    degree_hbm,
    weight_hbm,
    bias_hbm,
    features_hbm,
    tiles_hbm,
    out,
    slot_of,
    bias,
    degree,
    weight,
    scale,
    tiles,
    a_high,
    a_low,
    w_pair,
    raw,
    scales,
    first,
    field,
    total,
    partial_out,
    partial_in,
    load_sem,
    scale_send,
    scale_recv,
    raw_recv,
    z_send,
    x_send,
    y_send,
    pair_send,
    pair_recv,
    line_send,
    line_recv,
    out_send,
    out_recv,
):
    nodes, rels, chunks = sizes
    rows, depth = raw.shape[1:]
    row_tiles, slots, tile = tiles.shape[:3]
    width = chunks * LANES
    col_tiles = nodes * row_tiles
    group = rows // rels
    unit = tile // rels
    last = nodes - 1
    rel, node, feat = (lax.axis_index(name) for name in ("rel", "node", "feat"))
    has_up, has_down = node < last, node > 0
    x_rel, y_rel, far_rel = rel + 1 - 2 * lax.rem(rel, 2), lax.rem(rel + 2, rels), rels - 1 - rel
    owner = {"O": rel, "X": x_rel, "Y": y_rel, "F": far_rel}

    barrier = pltpu.get_barrier_semaphore()
    pl.semaphore_signal(barrier, inc=1, device_id={"feat": 1 - feat}, device_id_type=MESH)
    for step in range(1, rels):
        peer = lax.rem(rel + step, rels)
        pl.semaphore_signal(barrier, inc=1, device_id={"rel": peer}, device_id_type=MESH)
    for step in range(1, nodes):
        peer = lax.rem(node + step, nodes)
        pl.semaphore_signal(barrier, inc=1, device_id={"node": peer}, device_id_type=MESH)
    features_copy = pltpu.make_async_copy(features_hbm, raw.at[node], load_sem.at[0])
    degree_copy = pltpu.make_async_copy(degree_hbm, degree, load_sem.at[2])
    degree_copy.start()
    features_copy.start()
    bias_copy = pltpu.make_async_copy(bias_hbm, bias, load_sem.at[4])
    bias_copy.start()
    weight_copy = pltpu.make_async_copy(weight_hbm, weight, load_sem.at[3])
    weight_copy.start()
    tiles_copy = pltpu.make_async_copy(tiles_hbm, tiles, load_sem.at[1])
    tiles_copy.start()
    degree_copy.wait()
    row_scale = lax.rsqrt(degree[...].astype(jnp.float32))
    scales[node] = jnp.zeros(scales.shape[1:], jnp.float32)
    for t in range(row_tiles):
        scales[node, t : t + 1, :] = row_scale[:, t * tile : (t + 1) * tile]
    features_copy.wait()
    pl.semaphore_wait(barrier, rels + nodes - 1)

    def remote(src, dst, send_sem, recv_sem, **device):
        return pltpu.make_async_remote_copy(
            src_ref=src,
            dst_ref=dst,
            send_sem=send_sem,
            recv_sem=recv_sem,
            device_id=device,
            device_id_type=MESH,
        )

    def scale_copy(slot, step):
        peer = lax.rem(node + step, nodes)
        return remote(
            scales.at[slot], scales.at[slot], scale_send.at[step], scale_recv.at[slot], node=peer
        )

    def tile_rows(t):
        return pl.ds(pl.multiple_of(t * tile, tile), tile)

    def piece(slot, t, kind):
        start = pl.multiple_of(t * tile + owner[kind] * unit, unit)
        return raw.at[slot, pl.ds(start, unit), :], raw_recv.at[slot, t, owner[kind]]

    def z_copy(way, slot, kind, t):
        ref, recv_sem = piece(slot, t, kind)
        index = t if kind == "O" else Z_INDEX[kind, t]
        neighbour = node + 1 if way == 0 else node - 1
        return remote(ref, ref, z_send.at[way, slot, index], recv_sem, node=neighbour)

    def x_copy(slot, kind, t):
        ref, recv_sem = piece(slot, t, kind)
        index = t if kind == "O" else row_tiles
        return remote(ref, ref, x_send.at[slot, index], recv_sem, rel=x_rel)

    def y_copy(slot, kind, t):
        ref, recv_sem = piece(slot, t, kind)
        index = t if kind == "O" else row_tiles
        return remote(ref, ref, y_send.at[slot, index], recv_sem, rel=y_rel)

    def arrived(slot, kind, t):
        x_copy(slot, kind, t).wait_recv()

    def inner(i):
        return jnp.logical_and(i > 0, i < last)

    def is_end(i):
        return jnp.logical_or(i == 0, i == last)

    def plans(source, receiver, near):
        inside = jnp.logical_and(near, inner(receiver))
        rich = jnp.logical_and(inside, is_end(source))
        middle = jnp.logical_and(inside, inner(source))
        return rich, middle

    def exists(way, s):
        return node - s >= 0 if way == 0 else node + s < nodes

    def slot_at(way, s):
        return node - s if way == 0 else node + s

    def onward(way):
        return has_up if way == 0 else has_down

    def on_sides(s, act):
        for way in range(2):

            @pl.when(exists(way, s))
            def _(way=way):
                act(way, slot_at(way, s))

    def x_sends(slot, s):
        rich, middle = plans(slot, node, s == 1)
        plain = jnp.logical_not(jnp.logical_or(rich, middle))
        yield jnp.logical_not(rich), functools.partial(x_copy, slot, "O", 0)
        yield jnp.logical_not(rich), functools.partial(x_copy, slot, "O", 1)
        yield None, functools.partial(x_copy, slot, "O", 2)
        yield plain, functools.partial(x_copy, slot, "Y", 0)

    def y_sends(slot, s):
        rich, middle = plans(slot, node, s == 1)
        plain = jnp.logical_not(jnp.logical_or(rich, middle))
        yield jnp.logical_not(rich), functools.partial(y_copy, slot, "O", 0)
        yield jnp.logical_not(rich), functools.partial(y_copy, slot, "O", 1)
        yield None, functools.partial(y_copy, slot, "O", 2)
        yield plain, functools.partial(y_copy, slot, "X", 1)

    def z_extras(way):
        neighbour = node + 1 if way == 0 else node - 1
        rich, middle = plans(node, neighbour, True)
        more = jnp.logical_or(rich, middle)
        yield None, functools.partial(z_copy, way, node, "F", 2)
        yield more, functools.partial(z_copy, way, node, "F", 0)
        yield rich, functools.partial(z_copy, way, node, "X", 0)
        yield rich, functools.partial(z_copy, way, node, "Y", 0)
        yield more, functools.partial(z_copy, way, node, "F", 1)
        yield rich, functools.partial(z_copy, way, node, "X", 1)
        yield rich, functools.partial(z_copy, way, node, "Y", 1)

    def act_if(condition, act):
        if condition is None:
            act()
        else:
            pl.when(condition)(act)

    def take_own(s, t):
        def act(way, slot):
            arrived(slot, "O", t)

            @pl.when(onward(way))
            def _():
                z_copy(way, slot, "O", t).start()

            for sends in (x_sends, y_sends):
                condition, copy = list(sends(slot, s))[t]
                act_if(condition, lambda: copy().start())

        on_sides(s, act)

    def relay_x(way, slot, s):
        condition, copy = list(x_sends(slot, s))[3]

        @pl.when(condition)
        def _():
            arrived(slot, "Y", 0)
            copy().start()

    def relay_y(way, slot, s):
        condition, copy = list(y_sends(slot, s))[3]

        @pl.when(condition)
        def _():
            arrived(slot, "X", 1)
            copy().start()

    def relay_pending(s, relay):
        for way in range(2):

            @pl.when(both_and(exists(way, s), exists(way, s + 1)))
            def _(way=way):
                relay(way, slot_at(way, s), s)

    def relay_final(s):
        for way in range(2):

            @pl.when(both_and(exists(way, s), jnp.logical_not(exists(way, s + 1))))
            def _(way=way):
                relay_x(way, slot_at(way, s), s)
                relay_y(way, slot_at(way, s), s)

    def finish_raw(way, slot, s, t):
        rich, middle = plans(slot, node, s == 1)
        plain = jnp.logical_not(jnp.logical_or(rich, middle))
        if t == 2:
            arrived(slot, "F", 2)

            @pl.when(onward(way))
            def _():
                z_copy(way, slot, "F", 2).start()

            arrived(slot, "X", 2)
            arrived(slot, "Y", 2)
        elif t == 1:
            arrived(slot, "F", 1)
            arrived(slot, "Y", 1)
            act_if(jnp.logical_not(plain), lambda: arrived(slot, "X", 1))
        else:
            arrived(slot, "F", 0)
            arrived(slot, "X", 0)
            act_if(jnp.logical_not(plain), lambda: arrived(slot, "Y", 0))

    def add_products(acc, b_high, b_pair, column):
        for m in range(row_tiles):
            k = slot_of[m * col_tiles + column]
            acc[m * tile : (m + 1) * tile, :] += product(a_high[m, k], a_low[m, k], b_high, b_pair)

    def add_first(slot, t):
        b_high, b_low = split(raw[slot, tile_rows(t), :])
        add_products(first, b_high, jnp.concatenate([b_high, b_low], axis=1), slot * row_tiles + t)

    def prepare(t):
        def one(k, carry):
            c = tile_cols[t, 0, k]
            live = (k < tile_count[0, t]).astype(jnp.float32)
            column_scale = scales[lax.div(c, row_tiles), pl.ds(lax.rem(c, row_tiles), 1), :]
            high, low = split(tiles[t, k] * (column_scale * live))
            a_high[t, k] = high
            a_low[t, k] = low
            return carry

        lax.fori_loop(0, slots, one, 0)
        a_high[t, slots] = jnp.zeros((tile, tile), jnp.bfloat16)
        a_low[t, slots] = jnp.zeros((tile, tile), jnp.bfloat16)

    for step in range(1, nodes):
        scale_copy(node, step).start()
    for t in range(row_tiles):
        for way in range(2):

            @pl.when(onward(way))
            def _(way=way, t=t):
                z_copy(way, node, "O", t).start()

    def send_extras():
        for way in range(2):

            @pl.when(onward(way))
            def _(way=way):
                for condition, copy in z_extras(way):
                    act_if(condition, lambda: copy().start())

    pl.when(is_end(node))(send_extras)
    for t in range(row_tiles):

        def find(c, carry, t=t):
            found = jnp.int32(slots)
            for k in range(slots):
                found = jnp.where(tile_cols[t, 0, k] == c, k, found)
            slot_of[t * col_tiles + c] = found
            return carry

        lax.fori_loop(0, col_tiles, find, 0)
    bias_copy.wait()
    weight_copy.wait()
    w_high, w_low = split(weight[...])
    for side in range(2):
        w_pair[side, :, :width] = w_high[:, side * width : (side + 1) * width]
        w_pair[side, :, width:] = w_low[:, side * width : (side + 1) * width]
    for block in range(rows // LANES):
        lanes = slice(block * LANES, (block + 1) * LANES)
        scale[lanes, :] = jnp.broadcast_to(row_scale[:, lanes], (LANES, LANES)).T
    first[...] = jnp.zeros_like(first)
    total[...] = jnp.zeros_like(total)
    for step in range(1, nodes):
        scale_copy(lax.rem(node + step, nodes), 1).wait_recv()
    tiles_copy.wait()
    for t in range(row_tiles):
        prepare(t)
        take_own(1, t)
    pl.when(inner(node))(send_extras)
    if nodes <= 2:
        relay_final(1)

    def own_first(t, carry):
        add_first(node, t)
        return carry

    lax.fori_loop(0, row_tiles, own_first, 0)

    def use_raw(s):
        for t in (2, 0, 1):

            def act(way, slot, t=t):
                finish_raw(way, slot, s, t)
                add_first(slot, t)

            on_sides(s, act)

    def first_step(s, carry):
        @pl.when(s == 2)
        def _():
            for way in range(2):

                @pl.when(both_and(exists(way, 1), jnp.logical_not(exists(way, 2))))
                def _(way=way):
                    relay_x(way, slot_at(way, 1), 1)
                    relay_y(way, slot_at(way, 1), 1)

        take_own(s, 0)
        relay_pending(s - 1, relay_x)
        take_own(s, 1)
        relay_pending(s - 1, relay_y)
        take_own(s, 2)
        relay_final(s)
        use_raw(s - 1)
        return carry

    lax.fori_loop(2, nodes, first_step, 0)
    use_raw(last)

    def project(side, t):
        f_high, f_low = split(first[tile_rows(t), :])
        pair = w_pair[side]
        return product(f_high, f_low, pair[:, :width], pair)

    def pair_copy(t):
        return remote(
            partial_out.at[t], partial_in.at[t], pair_send.at[t], pair_recv.at[t], feat=1 - feat
        )

    def line_copy(chunk, way, slot, t):
        neighbour = node + 1 if way == 0 else node - 1
        ref = field.at[chunk, slot, tile_rows(t), :]
        return remote(
            ref,
            ref,
            line_send.at[chunk, way, slot, t],
            line_recv.at[chunk, slot, t],
            node=neighbour,
        )

    def add_field(chunk, slot, t):
        b_high, b_low = split(field[chunk, slot, tile_rows(t), :])
        column = slot * row_tiles + t
        add_products(total.at[chunk], b_high, jnp.concatenate([b_high, b_low], axis=1), column)

    def send_own(chunk, t):
        for way in range(2):

            @pl.when(onward(way))
            def _(way=way):
                line_copy(chunk, way, node, t).start()

    def take(chunk, s):
        def one(t, carry):
            def forward(way, slot):
                line_copy(chunk, way, slot, t).wait_recv()

                @pl.when(onward(way))
                def _():
                    line_copy(chunk, way, slot, t).start()

            on_sides(s, forward)
            on_sides(s, lambda way, slot: add_field(chunk, slot, t))
            return carry

        lax.fori_loop(0, row_tiles, one, 0)

    for t in range(row_tiles):
        partial_out[t] = project(1 - feat, t)
        pair_copy(t).start()
    for t in range(row_tiles):
        mine = project(feat, t)
        pair_copy(t).wait_recv()
        mine = mine + partial_in[t]
        for chunk in range(chunks):
            columns = slice(chunk * LANES, (chunk + 1) * LANES)
            row_slice = slice(t * tile, (t + 1) * tile)
            field[chunk, node, row_slice, :] = scale[row_slice, :] * mine[:, columns]
        send_own(0, t)

    def out_copy(chunk, step):
        peer = lax.rem(rel + step, rels)
        return remote(
            total.at[chunk, pl.ds(pl.multiple_of(peer * group, 8), group), :],
            out.at[rel, :, pl.ds(chunk * LANES, LANES)],
            out_send.at[chunk, step],
            out_recv.at[chunk, step],
            rel=peer,
        )

    def in_copy(chunk, step):
        peer = lax.rem(rel + rels - step, rels)
        return remote(
            total.at[chunk, pl.ds(0, group), :],
            out.at[peer, :, pl.ds(chunk * LANES, LANES)],
            out_send.at[chunk, step],
            out_recv.at[chunk, step],
            rel=peer,
        )

    def own_copy(chunk):
        return pltpu.make_async_copy(
            total.at[chunk, pl.ds(pl.multiple_of(rel * group, 8), group), :],
            out.at[rel, :, pl.ds(chunk * LANES, LANES)],
            load_sem.at[5 + chunk],
        )

    def finish(chunk):
        columns = slice(chunk * LANES, (chunk + 1) * LANES)
        total[chunk] = scale[...] * total[chunk] + bias[:, columns]
        for step in range(1, rels):
            out_copy(chunk, step).start()
        own_copy(chunk).start()

    def add_own(chunk):
        def one(t, carry):
            add_field(chunk, node, t)
            return carry

        lax.fori_loop(0, row_tiles, one, 0)

    for chunk in range(1, chunks):
        for t in range(row_tiles):
            send_own(chunk, t)
    for chunk in range(chunks):
        add_own(chunk)

    def hop_step(s, carry):
        for chunk in range(chunks):
            take(chunk, s)
        return carry

    lax.fori_loop(1, last, hop_step, 0)
    take(0, last)
    finish(0)

    def drain_raw(slot, carry):
        for way in range(2):
            mine = slot <= node if way == 0 else slot >= node

            @pl.when(both_and(onward(way), mine))
            def _(way=way):
                for t in range(row_tiles):
                    z_copy(way, slot, "O", t).wait_send()

            @pl.when(both_and(onward(way), mine, slot != node))
            def _(way=way):
                z_copy(way, slot, "F", 2).wait_send()

        @pl.when(slot != node)
        def _():
            s = jnp.abs(slot - node)
            for sends in (x_sends, y_sends):
                for condition, copy in sends(slot, s):
                    act_if(condition, lambda: copy().wait_send())

        return carry

    lax.fori_loop(0, nodes, drain_raw, 0)
    for way in range(2):

        @pl.when(onward(way))
        def _(way=way):
            for condition, copy in z_extras(way):
                act_if(condition, lambda: copy().wait_send())

    for step in range(1, nodes):
        scale_copy(node, step).wait_send()
    for t in range(row_tiles):
        pair_copy(t).wait_send()
    for chunk in range(1, chunks):
        take(chunk, last)
        finish(chunk)

    def drain_line(slot, carry):
        for way in range(2):
            mine = slot <= node if way == 0 else slot >= node

            @pl.when(both_and(onward(way), mine))
            def _(way=way):
                for chunk in range(chunks):
                    for t in range(row_tiles):
                        line_copy(chunk, way, slot, t).wait_send()

        return carry

    lax.fori_loop(0, nodes, drain_line, 0)
    for chunk in range(chunks):
        own_copy(chunk).wait()
        for step in range(1, rels):
            out_copy(chunk, step).wait_send()
            in_copy(chunk, step).wait_recv()


def on_device(
    nodes, rels, features, tile_values, tile_cols, tile_count, degree, proj_weight, proj_bias
):
    rows, depth = features.shape
    _, row_tiles, slots, tile, _ = tile_values.shape
    width = proj_bias.shape[1]
    chunks = width // LANES
    col_tiles = nodes * row_tiles
    hbm = pl.BlockSpec(memory_space=pl.ANY)
    smem = pl.BlockSpec(memory_space=pltpu.SMEM)
    dma = pltpu.SemaphoreType.DMA
    return pl.pallas_call(
        functools.partial(kernel, (nodes, rels, chunks)),
        out_shape=pltpu.VMEM((rels, rows // rels, width), jnp.float32),
        in_specs=[smem, smem] + [hbm] * 5,
        out_specs=hbm,
        scratch_shapes=[
            pltpu.SMEM((row_tiles * col_tiles,), jnp.int32),
            pltpu.VMEM((1, width), jnp.float32),
            pltpu.VMEM((1, rows), jnp.int32),
            pltpu.VMEM((depth, 2 * width), jnp.float32),
            pltpu.VMEM((rows, LANES), jnp.float32),
            pltpu.VMEM((row_tiles, slots, tile, tile), jnp.float32),
            pltpu.VMEM((row_tiles, slots + 1, tile, tile), jnp.bfloat16),
            pltpu.VMEM((row_tiles, slots + 1, tile, tile), jnp.bfloat16),
            pltpu.VMEM((2, depth, 2 * width), jnp.bfloat16),
            pltpu.VMEM((nodes, rows, depth), jnp.float32),
            pltpu.VMEM((nodes, SUBLANES, tile), jnp.float32),
            pltpu.VMEM((rows, depth), jnp.float32),
            pltpu.VMEM((chunks, nodes, rows, LANES), jnp.float32),
            pltpu.VMEM((chunks, rows, LANES), jnp.float32),
            pltpu.VMEM((row_tiles, tile, width), jnp.float32),
            pltpu.VMEM((row_tiles, tile, width), jnp.float32),
            dma((5 + chunks,)),
            dma((nodes,)),
            dma((nodes,)),
            dma((nodes, row_tiles, rels)),
            dma((2, nodes, 10)),
            dma((nodes, row_tiles + 1)),
            dma((nodes, row_tiles + 1)),
            dma((row_tiles,)),
            dma((row_tiles,)),
            dma((chunks, 2, nodes, row_tiles)),
            dma((chunks, nodes, row_tiles)),
            dma((chunks, rels)),
            dma((chunks, rels)),
        ],
        compiler_params=pltpu.CompilerParams(
            collective_id=0, has_side_effects=True, vmem_limit_bytes=60 << 20
        ),
    )(
        tile_cols.transpose(1, 0, 2),
        tile_count,
        degree,
        proj_weight[0],
        proj_bias,
        features,
        tile_values[0],
    )


def solution(mesh):
    return jax.shard_map(
        functools.partial(on_device, mesh.shape["node"], mesh.shape["rel"]),
        mesh=mesh,
        in_specs=(
            P("node", "feat"),
            P("rel", "node", None, None, None),
            P("rel", "node", None),
            P("rel", "node"),
            P("rel", "node"),
            P("rel", "feat", None),
            P("rel", "feat"),
        ),
        out_specs=P(None, ("node", "rel"), "feat"),
        check_vma=False,
    )
```

```python
import functools

import jax
import jax.numpy as jnp
from jax import lax
from jax.experimental import pallas as pl
from jax.experimental.pallas import tpu as pltpu
from jax.sharding import PartitionSpec as P

MESH = pl.DeviceIdType.MESH
LANES = 128
SUBLANES = 8
Z_INDEX = {("F", 0): 3, ("F", 1): 4, ("F", 2): 5, ("X", 0): 6, ("Y", 0): 7, ("X", 1): 8, ("Y", 1): 9}


def split(x):
    high = x.astype(jnp.bfloat16)
    return high, (x - high.astype(jnp.float32)).astype(jnp.bfloat16)


def dot(a, b):
    return jnp.dot(a, b, preferred_element_type=jnp.float32)


def product(a_high, a_low, b_high, b_pair):
    width = b_high.shape[1]
    both = dot(a_high, b_pair)
    return both[:, :width] + both[:, width:] + dot(a_low, b_high)


def both_and(*terms):
    return functools.reduce(jnp.logical_and, terms)


def kernel(
    sizes,
    tile_cols,
    tile_count,
    degree_hbm,
    weight_hbm,
    bias_hbm,
    features_hbm,
    tiles_hbm,
    out,
    slot_of,
    bias,
    degree,
    weight,
    scale,
    tiles,
    a_high,
    a_low,
    w_pair,
    raw,
    scales,
    first,
    field,
    total,
    partial_out,
    partial_in,
    b_pair,
    load_sem,
    scale_send,
    scale_recv,
    raw_recv,
    z_send,
    x_send,
    y_send,
    pair_send,
    pair_recv,
    line_send,
    line_recv,
    out_send,
    out_recv,
):
    nodes, rels, chunks = sizes
    rows, depth = raw.shape[1:]
    row_tiles, slots, tile = tiles.shape[:3]
    width = chunks * LANES
    col_tiles = nodes * row_tiles
    group = rows // rels
    unit = tile // rels
    last = nodes - 1
    rel, node, feat = (lax.axis_index(name) for name in ("rel", "node", "feat"))
    has_up, has_down = node < last, node > 0
    x_rel, y_rel, far_rel = rel + 1 - 2 * lax.rem(rel, 2), lax.rem(rel + 2, rels), rels - 1 - rel
    owner = {"O": rel, "X": x_rel, "Y": y_rel, "F": far_rel}

    barrier = pltpu.get_barrier_semaphore()
    pl.semaphore_signal(barrier, inc=1, device_id={"feat": 1 - feat}, device_id_type=MESH)
    for step in range(1, rels):
        peer = lax.rem(rel + step, rels)
        pl.semaphore_signal(barrier, inc=1, device_id={"rel": peer}, device_id_type=MESH)
    for step in range(1, nodes):
        peer = lax.rem(node + step, nodes)
        pl.semaphore_signal(barrier, inc=1, device_id={"node": peer}, device_id_type=MESH)
    features_copy = pltpu.make_async_copy(features_hbm, raw.at[node], load_sem.at[0])
    degree_copy = pltpu.make_async_copy(degree_hbm, degree, load_sem.at[2])
    degree_copy.start()
    features_copy.start()
    bias_copy = pltpu.make_async_copy(bias_hbm, bias, load_sem.at[4])
    bias_copy.start()
    weight_copy = pltpu.make_async_copy(weight_hbm, weight, load_sem.at[3])
    weight_copy.start()
    tiles_copy = pltpu.make_async_copy(tiles_hbm, tiles, load_sem.at[1])
    tiles_copy.start()
    degree_copy.wait()
    row_scale = lax.rsqrt(degree[...].astype(jnp.float32))
    scales[node] = jnp.zeros(scales.shape[1:], jnp.float32)
    for t in range(row_tiles):
        scales[node, t : t + 1, :] = row_scale[:, t * tile : (t + 1) * tile]
    features_copy.wait()
    pl.semaphore_wait(barrier, rels + nodes - 1)

    def remote(src, dst, send_sem, recv_sem, **device):
        return pltpu.make_async_remote_copy(
            src_ref=src,
            dst_ref=dst,
            send_sem=send_sem,
            recv_sem=recv_sem,
            device_id=device,
            device_id_type=MESH,
        )

    def scale_copy(slot, step):
        peer = lax.rem(node + step, nodes)
        return remote(
            scales.at[slot], scales.at[slot], scale_send.at[step], scale_recv.at[slot], node=peer
        )

    def tile_rows(t):
        return pl.ds(pl.multiple_of(t * tile, tile), tile)

    def piece(slot, t, kind):
        start = pl.multiple_of(t * tile + owner[kind] * unit, unit)
        return raw.at[slot, pl.ds(start, unit), :], raw_recv.at[slot, t, owner[kind]]

    def z_copy(way, slot, kind, t):
        ref, recv_sem = piece(slot, t, kind)
        index = t if kind == "O" else Z_INDEX[kind, t]
        neighbour = node + 1 if way == 0 else node - 1
        return remote(ref, ref, z_send.at[way, slot, index], recv_sem, node=neighbour)

    def x_copy(slot, kind, t):
        ref, recv_sem = piece(slot, t, kind)
        index = t if kind == "O" else row_tiles
        return remote(ref, ref, x_send.at[slot, index], recv_sem, rel=x_rel)

    def y_copy(slot, kind, t):
        ref, recv_sem = piece(slot, t, kind)
        index = t if kind == "O" else row_tiles
        return remote(ref, ref, y_send.at[slot, index], recv_sem, rel=y_rel)

    def arrived(slot, kind, t):
        x_copy(slot, kind, t).wait_recv()

    def inner(i):
        return jnp.logical_and(i > 0, i < last)

    def is_end(i):
        return jnp.logical_or(i == 0, i == last)

    def plans(source, receiver, near):
        inside = jnp.logical_and(near, inner(receiver))
        rich = jnp.logical_and(inside, is_end(source))
        middle = jnp.logical_and(inside, inner(source))
        return rich, middle

    def exists(way, s):
        return node - s >= 0 if way == 0 else node + s < nodes

    def slot_at(way, s):
        return node - s if way == 0 else node + s

    def onward(way):
        return has_up if way == 0 else has_down

    def on_sides(s, act):
        for way in range(2):

            @pl.when(exists(way, s))
            def _(way=way):
                act(way, slot_at(way, s))

    def x_sends(slot, s):
        rich, middle = plans(slot, node, s == 1)
        plain = jnp.logical_not(jnp.logical_or(rich, middle))
        yield jnp.logical_not(rich), functools.partial(x_copy, slot, "O", 0)
        yield jnp.logical_not(rich), functools.partial(x_copy, slot, "O", 1)
        yield None, functools.partial(x_copy, slot, "O", 2)
        yield plain, functools.partial(x_copy, slot, "Y", 0)

    def y_sends(slot, s):
        rich, middle = plans(slot, node, s == 1)
        plain = jnp.logical_not(jnp.logical_or(rich, middle))
        yield jnp.logical_not(rich), functools.partial(y_copy, slot, "O", 0)
        yield jnp.logical_not(rich), functools.partial(y_copy, slot, "O", 1)
        yield None, functools.partial(y_copy, slot, "O", 2)
        yield plain, functools.partial(y_copy, slot, "X", 1)

    def z_extras(way):
        neighbour = node + 1 if way == 0 else node - 1
        rich, middle = plans(node, neighbour, True)
        more = jnp.logical_or(rich, middle)
        yield None, functools.partial(z_copy, way, node, "F", 2)
        yield more, functools.partial(z_copy, way, node, "F", 0)
        yield rich, functools.partial(z_copy, way, node, "X", 0)
        yield rich, functools.partial(z_copy, way, node, "Y", 0)
        yield more, functools.partial(z_copy, way, node, "F", 1)
        yield rich, functools.partial(z_copy, way, node, "X", 1)
        yield rich, functools.partial(z_copy, way, node, "Y", 1)

    def act_if(condition, act):
        if condition is None:
            act()
        else:
            pl.when(condition)(act)

    def take_own(s, t, wait_for_relay=False):
        def act(way, slot):
            arrived(slot, "O", t)

            @pl.when(onward(way))
            def _():
                z_copy(way, slot, "O", t).start()

            condition, copy = list(y_sends(slot, s))[t]
            act_if(condition, lambda: copy().start())
            condition, copy = list(x_sends(slot, s))[t]
            if wait_for_relay:
                pending = exists(way, s + 1)
                condition = pending if condition is None else both_and(condition, pending)
            act_if(condition, lambda: copy().start())

        on_sides(s, act)

    def relay_x(way, slot, s):
        condition, copy = list(x_sends(slot, s))[3]

        @pl.when(condition)
        def _():
            arrived(slot, "Y", 0)
            copy().start()

    def relay_y(way, slot, s):
        condition, copy = list(y_sends(slot, s))[3]

        @pl.when(condition)
        def _():
            arrived(slot, "X", 1)
            copy().start()

    def relay_pending(s, relay):
        for way in range(2):

            @pl.when(both_and(exists(way, s), exists(way, s + 1)))
            def _(way=way):
                relay(way, slot_at(way, s), s)

    def relay_final(s, relay):
        for way in range(2):

            @pl.when(both_and(exists(way, s), jnp.logical_not(exists(way, s + 1))))
            def _(way=way):
                relay(way, slot_at(way, s), s)

    def relay_final_x(s):
        def relay(way, slot, s):
            relay_x(way, slot, s)
            x_copy(slot, "O", 2).start()

        relay_final(s, relay)

    def finish_raw(way, slot, s, t):
        rich, middle = plans(slot, node, s == 1)
        plain = jnp.logical_not(jnp.logical_or(rich, middle))
        if t == 2:
            arrived(slot, "F", 2)

            @pl.when(onward(way))
            def _():
                z_copy(way, slot, "F", 2).start()

            arrived(slot, "X", 2)
            arrived(slot, "Y", 2)
        elif t == 1:
            arrived(slot, "F", 1)
            arrived(slot, "Y", 1)
            act_if(jnp.logical_not(plain), lambda: arrived(slot, "X", 1))
        else:
            arrived(slot, "F", 0)
            arrived(slot, "X", 0)
            act_if(jnp.logical_not(plain), lambda: arrived(slot, "Y", 0))

    def add_products(acc, b_high, b_pair, column):
        for m in range(row_tiles):
            k = slot_of[m * col_tiles + column]
            acc[m * tile : (m + 1) * tile, :] += product(a_high[m, k], a_low[m, k], b_high, b_pair)

    def add_first(slot, t):
        b_high, b_low = split(raw[slot, tile_rows(t), :])
        add_products(first, b_high, jnp.concatenate([b_high, b_low], axis=1), slot * row_tiles + t)

    def prepare(t):
        def one(k, carry):
            c = tile_cols[t, 0, k]
            live = (k < tile_count[0, t]).astype(jnp.float32)
            column_scale = scales[lax.div(c, row_tiles), pl.ds(lax.rem(c, row_tiles), 1), :]
            high, low = split(tiles[t, k] * (column_scale * live))
            a_high[t, k] = high
            a_low[t, k] = low
            return carry

        lax.fori_loop(0, slots, one, 0)
        a_high[t, slots] = jnp.zeros((tile, tile), jnp.bfloat16)
        a_low[t, slots] = jnp.zeros((tile, tile), jnp.bfloat16)

    for step in range(1, nodes):
        scale_copy(node, step).start()
    for t in range(row_tiles):
        for way in range(2):

            @pl.when(onward(way))
            def _(way=way, t=t):
                z_copy(way, node, "O", t).start()

    def send_extras():
        for way in range(2):

            @pl.when(onward(way))
            def _(way=way):
                for condition, copy in z_extras(way):
                    act_if(condition, lambda: copy().start())

    pl.when(is_end(node))(send_extras)
    for t in range(row_tiles):

        def find(c, carry, t=t):
            found = jnp.int32(slots)
            for k in range(slots):
                found = jnp.where(tile_cols[t, 0, k] == c, k, found)
            slot_of[t * col_tiles + c] = found
            return carry

        lax.fori_loop(0, col_tiles, find, 0)
    bias_copy.wait()
    weight_copy.wait()
    w_high, w_low = split(weight[...])
    for side in range(2):
        w_pair[side, :, :width] = w_high[:, side * width : (side + 1) * width]
        w_pair[side, :, width:] = w_low[:, side * width : (side + 1) * width]
    for block in range(rows // LANES):
        lanes = slice(block * LANES, (block + 1) * LANES)
        scale[lanes, :] = jnp.broadcast_to(row_scale[:, lanes], (LANES, LANES)).T
    first[...] = jnp.zeros_like(first)
    total[...] = jnp.zeros_like(total)
    for step in range(1, nodes):
        scale_copy(lax.rem(node + step, nodes), 1).wait_recv()
    tiles_copy.wait()
    for t in range(row_tiles):
        prepare(t)
        take_own(1, t)
    pl.when(inner(node))(send_extras)

    def own_first(t, carry):
        add_first(node, t)
        return carry

    lax.fori_loop(0, row_tiles, own_first, 0)

    far_slot = jnp.where(2 * node < nodes, last, 0)
    second_slot = jnp.where(node == 1, 0, jnp.where(node == last - 1, last, far_slot))
    if nodes <= 2:
        second_slot = far_slot

    def finish_at(slot, t):
        @pl.when(slot > node)
        def _():
            finish_raw(1, slot, slot - node, t)

        @pl.when(slot < node)
        def _():
            finish_raw(0, slot, node - slot, t)

    def use(s, t, which=None):
        def act(way, slot):
            now = jnp.bool_(True)
            if t == 2:
                now = slot != far_slot
            elif t == 1:
                now = slot != second_slot
            if which is not None:
                rich, _ = plans(slot, node, s == 1)
                now = both_and(now, rich if which == "rich" else jnp.logical_not(rich))

            @pl.when(now)
            def _():
                finish_raw(way, slot, s, t)
                add_first(slot, t)

        on_sides(s, act)

    def take_step(s):
        take_own(s, 0)
        relay_pending(s - 1, relay_x)
        take_own(s, 1)
        relay_pending(s - 1, relay_y)
        take_own(s, 2, wait_for_relay=True)

    def use_late(s):
        use(s, 0)
        use(s, 1)
        pl.when(s == 2)(lambda: use(1, 1, "rich"))
        use(s, 2)

    def late_step(s, carry):
        take_step(s)
        relay_final_x(s)
        relay_final(s, relay_y)
        use_late(s - 1)
        return carry

    if nodes > 2:
        take_step(2)
        use(1, 2, "rich")
        relay_final_x(2)
        use(1, 0, "rich")
        use(1, 2, "other")
        relay_final(2, relay_y)
        use(1, 0, "other")
        use(1, 1, "other")
        lax.fori_loop(3, nodes, late_step, 0)
        use_late(last)
    else:
        relay_final(1, relay_x)
        relay_final(1, relay_y)
        for t in range(row_tiles):
            use(1, t)

    def project(side, t):
        f_high, f_low = split(first[tile_rows(t), :])
        pair = w_pair[side]
        return product(f_high, f_low, pair[:, :width], pair)

    def pair_copy(t):
        return remote(
            partial_out.at[t], partial_in.at[t], pair_send.at[t], pair_recv.at[t], feat=1 - feat
        )

    def line_copy(chunk, way, slot, t):
        neighbour = node + 1 if way == 0 else node - 1
        ref = field.at[chunk, slot, tile_rows(t), :]
        return remote(
            ref,
            ref,
            line_send.at[chunk, way, slot, t],
            line_recv.at[chunk, slot, t],
            node=neighbour,
        )

    def add_field(chunk, slot, t):
        b_high, b_low = split(field[chunk, slot, tile_rows(t), :])
        column = slot * row_tiles + t
        add_products(total.at[chunk], b_high, jnp.concatenate([b_high, b_low], axis=1), column)

    def send_own(chunk, t):
        for way in range(2):

            @pl.when(onward(way))
            def _(way=way):
                line_copy(chunk, way, node, t).start()

    def take(chunk, s):
        def one(t, carry):
            def forward(way, slot):
                line_copy(chunk, way, slot, t).wait_recv()

                @pl.when(onward(way))
                def _():
                    line_copy(chunk, way, slot, t).start()

            on_sides(s, forward)
            on_sides(s, lambda way, slot: add_field(chunk, slot, t))
            return carry

        lax.fori_loop(0, row_tiles, one, 0)

    finals = ((second_slot, 1), (far_slot, 2))
    for n, (slot, t) in enumerate(finals):
        finish_at(slot, t)
        b_high, b_low = split(raw[slot, tile_rows(t), :])
        b_pair[n, :, :depth] = b_high
        b_pair[n, :, depth:] = b_low

    def give(m):
        rows_m = slice(m * tile, (m + 1) * tile)
        for n, (slot, t) in enumerate(finals):
            k = slot_of[m * col_tiles + slot * row_tiles + t]
            b = b_pair[n]
            first[rows_m, :] += product(a_high[m, k], a_low[m, k], b[:, :depth], b)
        partial_out[m] = project(1 - feat, m)
        pair_copy(m).start()

    def keep(m):
        mine = project(feat, m)
        pair_copy(m).wait_recv()
        mine = mine + partial_in[m]
        for chunk in range(chunks):
            columns = slice(chunk * LANES, (chunk + 1) * LANES)
            rows_m = slice(m * tile, (m + 1) * tile)
            field[chunk, node, rows_m, :] = scale[rows_m, :] * mine[:, columns]
        pl.when(feat == 0)(lambda: send_own(0, m))

    give(0)
    for m in range(row_tiles):
        if m + 1 < row_tiles:
            give(m + 1)
        keep(m)

    def out_copy(chunk, step):
        peer = lax.rem(rel + step, rels)
        return remote(
            total.at[chunk, pl.ds(pl.multiple_of(peer * group, 8), group), :],
            out.at[rel, :, pl.ds(chunk * LANES, LANES)],
            out_send.at[chunk, step],
            out_recv.at[chunk, step],
            rel=peer,
        )

    def in_copy(chunk, step):
        peer = lax.rem(rel + rels - step, rels)
        return remote(
            total.at[chunk, pl.ds(0, group), :],
            out.at[peer, :, pl.ds(chunk * LANES, LANES)],
            out_send.at[chunk, step],
            out_recv.at[chunk, step],
            rel=peer,
        )

    def own_copy(chunk):
        return pltpu.make_async_copy(
            total.at[chunk, pl.ds(pl.multiple_of(rel * group, 8), group), :],
            out.at[rel, :, pl.ds(chunk * LANES, LANES)],
            load_sem.at[5 + chunk],
        )

    def finish(chunk):
        columns = slice(chunk * LANES, (chunk + 1) * LANES)
        total[chunk] = scale[...] * total[chunk] + bias[:, columns]
        for step in range(1, rels):
            out_copy(chunk, step).start()
        own_copy(chunk).start()

    def add_own(chunk):
        def one(t, carry):
            add_field(chunk, node, t)
            return carry

        lax.fori_loop(0, row_tiles, one, 0)

    def send_rest(first_chunk):
        for chunk in range(first_chunk, chunks):
            for t in range(row_tiles):
                send_own(chunk, t)

    pl.when(feat == 0)(lambda: send_rest(1))
    for chunk in range(chunks):
        add_own(chunk)
    pl.when(feat != 0)(lambda: send_rest(0))

    def hop_step(s, carry):
        for chunk in range(chunks):
            take(chunk, s)
        return carry

    lax.fori_loop(1, last, hop_step, 0)
    take(0, last)
    finish(0)

    def drain_raw(slot, carry):
        for way in range(2):
            mine = slot <= node if way == 0 else slot >= node

            @pl.when(both_and(onward(way), mine))
            def _(way=way):
                for t in range(row_tiles):
                    z_copy(way, slot, "O", t).wait_send()

            @pl.when(both_and(onward(way), mine, slot != node))
            def _(way=way):
                z_copy(way, slot, "F", 2).wait_send()

        @pl.when(slot != node)
        def _():
            s = jnp.abs(slot - node)
            for sends in (x_sends, y_sends):
                for condition, copy in sends(slot, s):
                    act_if(condition, lambda: copy().wait_send())

        return carry

    lax.fori_loop(0, nodes, drain_raw, 0)
    for way in range(2):

        @pl.when(onward(way))
        def _(way=way):
            for condition, copy in z_extras(way):
                act_if(condition, lambda: copy().wait_send())

    for step in range(1, nodes):
        scale_copy(node, step).wait_send()
    for t in range(row_tiles):
        pair_copy(t).wait_send()
    for chunk in range(1, chunks):
        take(chunk, last)
        finish(chunk)

    def drain_line(slot, carry):
        for way in range(2):
            mine = slot <= node if way == 0 else slot >= node

            @pl.when(both_and(onward(way), mine))
            def _(way=way):
                for chunk in range(chunks):
                    for t in range(row_tiles):
                        line_copy(chunk, way, slot, t).wait_send()

        return carry

    lax.fori_loop(0, nodes, drain_line, 0)
    for chunk in range(chunks):
        own_copy(chunk).wait()
        for step in range(1, rels):
            out_copy(chunk, step).wait_send()
            in_copy(chunk, step).wait_recv()


def on_device(
    nodes, rels, features, tile_values, tile_cols, tile_count, degree, proj_weight, proj_bias
):
    rows, depth = features.shape
    _, row_tiles, slots, tile, _ = tile_values.shape
    width = proj_bias.shape[1]
    chunks = width // LANES
    col_tiles = nodes * row_tiles
    hbm = pl.BlockSpec(memory_space=pl.ANY)
    smem = pl.BlockSpec(memory_space=pltpu.SMEM)
    dma = pltpu.SemaphoreType.DMA
    return pl.pallas_call(
        functools.partial(kernel, (nodes, rels, chunks)),
        out_shape=pltpu.VMEM((rels, rows // rels, width), jnp.float32),
        in_specs=[smem, smem] + [hbm] * 5,
        out_specs=hbm,
        scratch_shapes=[
            pltpu.SMEM((row_tiles * col_tiles,), jnp.int32),
            pltpu.VMEM((1, width), jnp.float32),
            pltpu.VMEM((1, rows), jnp.int32),
            pltpu.VMEM((depth, 2 * width), jnp.float32),
            pltpu.VMEM((rows, LANES), jnp.float32),
            pltpu.VMEM((row_tiles, slots, tile, tile), jnp.float32),
            pltpu.VMEM((row_tiles, slots + 1, tile, tile), jnp.bfloat16),
            pltpu.VMEM((row_tiles, slots + 1, tile, tile), jnp.bfloat16),
            pltpu.VMEM((2, depth, 2 * width), jnp.bfloat16),
            pltpu.VMEM((nodes, rows, depth), jnp.float32),
            pltpu.VMEM((nodes, SUBLANES, tile), jnp.float32),
            pltpu.VMEM((rows, depth), jnp.float32),
            pltpu.VMEM((chunks, nodes, rows, LANES), jnp.float32),
            pltpu.VMEM((chunks, rows, LANES), jnp.float32),
            pltpu.VMEM((row_tiles, tile, width), jnp.float32),
            pltpu.VMEM((row_tiles, tile, width), jnp.float32),
            pltpu.VMEM((2, tile, 2 * depth), jnp.bfloat16),
            dma((5 + chunks,)),
            dma((nodes,)),
            dma((nodes,)),
            dma((nodes, row_tiles, rels)),
            dma((2, nodes, 10)),
            dma((nodes, row_tiles + 1)),
            dma((nodes, row_tiles + 1)),
            dma((row_tiles,)),
            dma((row_tiles,)),
            dma((chunks, 2, nodes, row_tiles)),
            dma((chunks, nodes, row_tiles)),
            dma((chunks, rels)),
            dma((chunks, rels)),
        ],
        compiler_params=pltpu.CompilerParams(
            collective_id=0, has_side_effects=True, vmem_limit_bytes=60 << 20
        ),
    )(
        tile_cols.transpose(1, 0, 2),
        tile_count,
        degree,
        proj_weight[0],
        proj_bias,
        features,
        tile_values[0],
    )


def solution(mesh):
    return jax.shard_map(
        functools.partial(on_device, mesh.shape["node"], mesh.shape["rel"]),
        mesh=mesh,
        in_specs=(
            P("node", "feat"),
            P("rel", "node", None, None, None),
            P("rel", "node", None),
            P("rel", "node"),
            P("rel", "node"),
            P("rel", "feat", None),
            P("rel", "feat"),
        ),
        out_specs=P(None, ("node", "rel"), "feat"),
        check_vma=False,
    )
```

```python
import functools

import jax
import jax.numpy as jnp
from jax import lax
from jax.experimental import pallas as pl
from jax.experimental.pallas import tpu as pltpu
from jax.sharding import PartitionSpec as P

MESH = pl.DeviceIdType.MESH
LANES = 128
SUBLANES = 8
Z_INDEX = {("F", 0): 3, ("F", 1): 4, ("F", 2): 5, ("X", 0): 6, ("Y", 0): 7, ("X", 1): 8, ("Y", 1): 9}


def split(x):
    high = x.astype(jnp.bfloat16)
    return high, (x - high.astype(jnp.float32)).astype(jnp.bfloat16)


def dot(a, b):
    return jnp.dot(a, b, preferred_element_type=jnp.float32)


def product(a_high, a_low, b_high, b_pair):
    width = b_high.shape[1]
    both = dot(a_high, b_pair)
    return both[:, :width] + both[:, width:] + dot(a_low, b_high)


def both_and(*terms):
    return functools.reduce(jnp.logical_and, terms)


def kernel(
    sizes,
    tile_cols,
    tile_count,
    degree_hbm,
    weight_hbm,
    bias_hbm,
    features_hbm,
    tiles_hbm,
    out,
    slot_of,
    bias,
    degree,
    weight,
    scale,
    tiles,
    a_high,
    a_low,
    w_pair,
    raw,
    scales,
    first,
    field,
    total,
    partial_out,
    partial_in,
    b_pair,
    load_sem,
    scale_send,
    scale_recv,
    raw_recv,
    z_send,
    x_send,
    y_send,
    pair_send,
    pair_recv,
    line_send,
    line_recv,
    out_send,
    out_recv,
):
    nodes, rels, chunks = sizes
    rows, depth = raw.shape[1:]
    row_tiles, slots, tile = tiles.shape[:3]
    width = chunks * LANES
    col_tiles = nodes * row_tiles
    group = rows // rels
    unit = tile // rels
    last = nodes - 1
    rel, node, feat = (lax.axis_index(name) for name in ("rel", "node", "feat"))
    has_up, has_down = node < last, node > 0
    x_rel, y_rel, far_rel = rel + 1 - 2 * lax.rem(rel, 2), lax.rem(rel + 2, rels), rels - 1 - rel
    owner = {"O": rel, "X": x_rel, "Y": y_rel, "F": far_rel}

    barrier = pltpu.get_barrier_semaphore()
    pl.semaphore_signal(barrier, inc=1, device_id={"feat": 1 - feat}, device_id_type=MESH)
    for step in range(1, rels):
        peer = lax.rem(rel + step, rels)
        pl.semaphore_signal(barrier, inc=1, device_id={"rel": peer}, device_id_type=MESH)
    for step in range(1, nodes):
        peer = lax.rem(node + step, nodes)
        pl.semaphore_signal(barrier, inc=1, device_id={"node": peer}, device_id_type=MESH)
    features_copy = pltpu.make_async_copy(features_hbm, raw.at[node], load_sem.at[0])
    degree_copy = pltpu.make_async_copy(degree_hbm, degree, load_sem.at[2])
    degree_copy.start()
    features_copy.start()
    bias_copy = pltpu.make_async_copy(bias_hbm, bias, load_sem.at[4])
    bias_copy.start()
    weight_copy = pltpu.make_async_copy(weight_hbm, weight, load_sem.at[3])
    weight_copy.start()
    tiles_copy = pltpu.make_async_copy(tiles_hbm, tiles, load_sem.at[1])
    tiles_copy.start()
    degree_copy.wait()
    row_scale = lax.rsqrt(degree[...].astype(jnp.float32))
    scales[node] = jnp.zeros(scales.shape[1:], jnp.float32)
    for t in range(row_tiles):
        scales[node, t : t + 1, :] = row_scale[:, t * tile : (t + 1) * tile]
    features_copy.wait()
    pl.semaphore_wait(barrier, rels + nodes - 1)

    def remote(src, dst, send_sem, recv_sem, **device):
        return pltpu.make_async_remote_copy(
            src_ref=src,
            dst_ref=dst,
            send_sem=send_sem,
            recv_sem=recv_sem,
            device_id=device,
            device_id_type=MESH,
        )

    def scale_copy(slot, step):
        peer = lax.rem(node + step, nodes)
        return remote(
            scales.at[slot], scales.at[slot], scale_send.at[step], scale_recv.at[slot], node=peer
        )

    def tile_rows(t):
        return pl.ds(pl.multiple_of(t * tile, tile), tile)

    def piece(slot, t, kind):
        start = pl.multiple_of(t * tile + owner[kind] * unit, unit)
        return raw.at[slot, pl.ds(start, unit), :], raw_recv.at[slot, t, owner[kind]]

    def z_copy(way, slot, kind, t):
        ref, recv_sem = piece(slot, t, kind)
        index = t if kind == "O" else Z_INDEX[kind, t]
        neighbour = node + 1 if way == 0 else node - 1
        return remote(ref, ref, z_send.at[way, slot, index], recv_sem, node=neighbour)

    def x_copy(slot, kind, t):
        ref, recv_sem = piece(slot, t, kind)
        index = t if kind == "O" else row_tiles
        return remote(ref, ref, x_send.at[slot, index], recv_sem, rel=x_rel)

    def y_copy(slot, kind, t):
        ref, recv_sem = piece(slot, t, kind)
        index = t if kind == "O" else row_tiles
        return remote(ref, ref, y_send.at[slot, index], recv_sem, rel=y_rel)

    def arrived(slot, kind, t):
        x_copy(slot, kind, t).wait_recv()

    def inner(i):
        return jnp.logical_and(i > 0, i < last)

    def is_end(i):
        return jnp.logical_or(i == 0, i == last)

    def plans(source, receiver, near):
        inside = jnp.logical_and(near, inner(receiver))
        rich = jnp.logical_and(inside, is_end(source))
        middle = jnp.logical_and(inside, inner(source))
        return rich, middle

    def exists(way, s):
        return node - s >= 0 if way == 0 else node + s < nodes

    def slot_at(way, s):
        return node - s if way == 0 else node + s

    def onward(way):
        return has_up if way == 0 else has_down

    def on_sides(s, act):
        for way in range(2):

            @pl.when(exists(way, s))
            def _(way=way):
                act(way, slot_at(way, s))

    def x_sends(slot, s):
        rich, middle = plans(slot, node, s == 1)
        plain = jnp.logical_not(jnp.logical_or(rich, middle))
        yield jnp.logical_not(rich), functools.partial(x_copy, slot, "O", 0)
        yield jnp.logical_not(rich), functools.partial(x_copy, slot, "O", 1)
        yield None, functools.partial(x_copy, slot, "O", 2)
        yield plain, functools.partial(x_copy, slot, "Y", 0)

    def y_sends(slot, s):
        rich, middle = plans(slot, node, s == 1)
        plain = jnp.logical_not(jnp.logical_or(rich, middle))
        yield jnp.logical_not(rich), functools.partial(y_copy, slot, "O", 0)
        yield jnp.logical_not(rich), functools.partial(y_copy, slot, "O", 1)
        yield None, functools.partial(y_copy, slot, "O", 2)
        yield plain, functools.partial(y_copy, slot, "X", 1)

    def z_extras(way):
        neighbour = node + 1 if way == 0 else node - 1
        rich, middle = plans(node, neighbour, True)
        more = jnp.logical_or(rich, middle)
        yield None, functools.partial(z_copy, way, node, "F", 2)
        yield more, functools.partial(z_copy, way, node, "F", 0)
        yield rich, functools.partial(z_copy, way, node, "X", 0)
        yield rich, functools.partial(z_copy, way, node, "Y", 0)
        yield more, functools.partial(z_copy, way, node, "F", 1)
        yield rich, functools.partial(z_copy, way, node, "X", 1)
        yield rich, functools.partial(z_copy, way, node, "Y", 1)

    def act_if(condition, act):
        if condition is None:
            act()
        else:
            pl.when(condition)(act)

    def take_own(s, t, wait_for_relay=False):
        def act(way, slot):
            arrived(slot, "O", t)

            @pl.when(onward(way))
            def _():
                z_copy(way, slot, "O", t).start()

            condition, copy = list(y_sends(slot, s))[t]
            act_if(condition, lambda: copy().start())
            condition, copy = list(x_sends(slot, s))[t]
            if wait_for_relay:
                pending = exists(way, s + 1)
                condition = pending if condition is None else both_and(condition, pending)
            act_if(condition, lambda: copy().start())

        on_sides(s, act)

    def relay_x(way, slot, s):
        condition, copy = list(x_sends(slot, s))[3]

        @pl.when(condition)
        def _():
            arrived(slot, "Y", 0)
            copy().start()

    def relay_y(way, slot, s):
        condition, copy = list(y_sends(slot, s))[3]

        @pl.when(condition)
        def _():
            arrived(slot, "X", 1)
            copy().start()

    def relay_pending(s, relay):
        for way in range(2):

            @pl.when(both_and(exists(way, s), exists(way, s + 1)))
            def _(way=way):
                relay(way, slot_at(way, s), s)

    def relay_final(s, relay):
        for way in range(2):

            @pl.when(both_and(exists(way, s), jnp.logical_not(exists(way, s + 1))))
            def _(way=way):
                relay(way, slot_at(way, s), s)

    def relay_final_x(s):
        def relay(way, slot, s):
            relay_x(way, slot, s)
            x_copy(slot, "O", 2).start()

        relay_final(s, relay)

    def finish_raw(way, slot, s, t):
        rich, middle = plans(slot, node, s == 1)
        plain = jnp.logical_not(jnp.logical_or(rich, middle))
        if t == 2:
            arrived(slot, "F", 2)

            @pl.when(onward(way))
            def _():
                z_copy(way, slot, "F", 2).start()

            arrived(slot, "X", 2)
            arrived(slot, "Y", 2)
        elif t == 1:
            arrived(slot, "F", 1)
            arrived(slot, "Y", 1)
            act_if(jnp.logical_not(plain), lambda: arrived(slot, "X", 1))
        else:
            arrived(slot, "F", 0)
            arrived(slot, "X", 0)
            act_if(jnp.logical_not(plain), lambda: arrived(slot, "Y", 0))

    def add_products(acc, b_high, b_pair, column):
        for m in range(row_tiles):
            k = slot_of[m * col_tiles + column]
            acc[m * tile : (m + 1) * tile, :] += product(a_high[m, k], a_low[m, k], b_high, b_pair)

    def add_first(slot, t):
        b_high, b_low = split(raw[slot, tile_rows(t), :])
        add_products(first, b_high, jnp.concatenate([b_high, b_low], axis=1), slot * row_tiles + t)

    def prepare(t):
        def one(k, carry):
            c = tile_cols[t, 0, k]
            live = (k < tile_count[0, t]).astype(jnp.float32)
            column_scale = scales[lax.div(c, row_tiles), pl.ds(lax.rem(c, row_tiles), 1), :]
            high, low = split(tiles[t, k] * (column_scale * live))
            a_high[t, k] = high
            a_low[t, k] = low
            return carry

        lax.fori_loop(0, slots, one, 0)
        a_high[t, slots] = jnp.zeros((tile, tile), jnp.bfloat16)
        a_low[t, slots] = jnp.zeros((tile, tile), jnp.bfloat16)

    for step in range(1, nodes):
        scale_copy(node, step).start()
    for t in range(row_tiles):
        for way in range(2):

            @pl.when(onward(way))
            def _(way=way, t=t):
                z_copy(way, node, "O", t).start()

    def send_extras():
        for way in range(2):

            @pl.when(onward(way))
            def _(way=way):
                for condition, copy in z_extras(way):
                    act_if(condition, lambda: copy().start())

    pl.when(is_end(node))(send_extras)
    for t in range(row_tiles):

        def find(c, carry, t=t):
            found = jnp.int32(slots)
            for k in range(slots):
                found = jnp.where(tile_cols[t, 0, k] == c, k, found)
            slot_of[t * col_tiles + c] = found
            return carry

        lax.fori_loop(0, col_tiles, find, 0)
    bias_copy.wait()
    weight_copy.wait()
    w_high, w_low = split(weight[...])
    for side in range(2):
        w_pair[side, :, :width] = w_high[:, side * width : (side + 1) * width]
        w_pair[side, :, width:] = w_low[:, side * width : (side + 1) * width]
    for block in range(rows // LANES):
        lanes = slice(block * LANES, (block + 1) * LANES)
        scale[lanes, :] = jnp.broadcast_to(row_scale[:, lanes], (LANES, LANES)).T
    first[...] = jnp.zeros_like(first)
    total[...] = jnp.zeros_like(total)
    take_own(1, 0)
    for step in range(1, nodes):
        scale_copy(lax.rem(node + step, nodes), 1).wait_recv()
    tiles_copy.wait()
    for t in range(row_tiles):
        prepare(t)
        if t + 1 < row_tiles:
            take_own(1, t + 1)
    pl.when(inner(node))(send_extras)

    def own_first(t, carry):
        add_first(node, t)
        return carry

    lax.fori_loop(0, row_tiles, own_first, 0)

    far_slot = jnp.where(2 * node < nodes, last, 0)
    second_slot = jnp.where(node == 1, 0, jnp.where(node == last - 1, last, far_slot))
    if nodes <= 2:
        second_slot = far_slot

    def finish_at(slot, t):
        @pl.when(slot > node)
        def _():
            finish_raw(1, slot, slot - node, t)

        @pl.when(slot < node)
        def _():
            finish_raw(0, slot, node - slot, t)

    def use(s, t, which=None):
        def act(way, slot):
            now = jnp.bool_(True)
            if t == 2:
                now = slot != far_slot
            elif t == 1:
                now = slot != second_slot
            if which is not None:
                rich, _ = plans(slot, node, s == 1)
                now = both_and(now, rich if which == "rich" else jnp.logical_not(rich))

            @pl.when(now)
            def _():
                finish_raw(way, slot, s, t)
                add_first(slot, t)

        on_sides(s, act)

    def take_step(s):
        take_own(s, 0)
        relay_pending(s - 1, relay_x)
        take_own(s, 1)
        relay_pending(s - 1, relay_y)
        take_own(s, 2, wait_for_relay=True)

    def use_late(s):
        use(s, 0)
        use(s, 1)
        pl.when(s == 2)(lambda: use(1, 1, "rich"))
        use(s, 2)

    def late_step(s, carry):
        take_step(s)
        relay_final_x(s)
        relay_final(s, relay_y)
        use_late(s - 1)
        return carry

    if nodes > 2:
        take_step(2)
        use(1, 2, "rich")
        relay_final_x(2)
        use(1, 0, "rich")
        use(1, 2, "other")
        relay_final(2, relay_y)
        use(1, 0, "other")
        use(1, 1, "other")
        lax.fori_loop(3, nodes, late_step, 0)
        use_late(last)
    else:
        relay_final(1, relay_x)
        relay_final(1, relay_y)
        for t in range(row_tiles):
            use(1, t)

    def project(side, t):
        f_high, f_low = split(first[tile_rows(t), :])
        pair = w_pair[side]
        return product(f_high, f_low, pair[:, :width], pair)

    def pair_copy(t):
        return remote(
            partial_out.at[t], partial_in.at[t], pair_send.at[t], pair_recv.at[t], feat=1 - feat
        )

    def line_copy(chunk, way, slot, t):
        neighbour = node + 1 if way == 0 else node - 1
        ref = field.at[chunk, slot, tile_rows(t), :]
        return remote(
            ref,
            ref,
            line_send.at[chunk, way, slot, t],
            line_recv.at[chunk, slot, t],
            node=neighbour,
        )

    def add_field(chunk, slot, t):
        b_high, b_low = split(field[chunk, slot, tile_rows(t), :])
        column = slot * row_tiles + t
        add_products(total.at[chunk], b_high, jnp.concatenate([b_high, b_low], axis=1), column)

    def send_own(chunk, t):
        for way in range(2):

            @pl.when(onward(way))
            def _(way=way):
                line_copy(chunk, way, node, t).start()

    def take(chunk, s):
        def one(t, carry):
            def forward(way, slot):
                line_copy(chunk, way, slot, t).wait_recv()

                @pl.when(onward(way))
                def _():
                    line_copy(chunk, way, slot, t).start()

            on_sides(s, forward)
            on_sides(s, lambda way, slot: add_field(chunk, slot, t))
            return carry

        lax.fori_loop(0, row_tiles, one, 0)

    finals = ((second_slot, 1), (far_slot, 2))
    for n, (slot, t) in enumerate(finals):
        finish_at(slot, t)
        b_high, b_low = split(raw[slot, tile_rows(t), :])
        b_pair[n, :, :depth] = b_high
        b_pair[n, :, depth:] = b_low

    def give(m):
        rows_m = slice(m * tile, (m + 1) * tile)
        for n, (slot, t) in enumerate(finals):
            k = slot_of[m * col_tiles + slot * row_tiles + t]
            b = b_pair[n]
            first[rows_m, :] += product(a_high[m, k], a_low[m, k], b[:, :depth], b)
        partial_out[m] = project(1 - feat, m)
        pair_copy(m).start()

    def keep(m):
        mine = project(feat, m)
        pair_copy(m).wait_recv()
        mine = mine + partial_in[m]
        for chunk in range(chunks):
            columns = slice(chunk * LANES, (chunk + 1) * LANES)
            rows_m = slice(m * tile, (m + 1) * tile)
            field[chunk, node, rows_m, :] = scale[rows_m, :] * mine[:, columns]
        pl.when(feat == 0)(lambda: send_own(0, m))

    give(0)
    for m in range(row_tiles):
        if m + 1 < row_tiles:
            give(m + 1)
        keep(m)

    def out_copy(chunk, step):
        peer = (x_rel, y_rel, far_rel)[step - 1]
        return remote(
            total.at[chunk, pl.ds(pl.multiple_of(peer * group, 8), group), :],
            out.at[rel, :, pl.ds(chunk * LANES, LANES)],
            out_send.at[chunk, step],
            out_recv.at[chunk, step],
            rel=peer,
        )

    def in_copy(chunk, step):
        peer = (x_rel, y_rel, far_rel)[step - 1]
        return remote(
            total.at[chunk, pl.ds(0, group), :],
            out.at[peer, :, pl.ds(chunk * LANES, LANES)],
            out_send.at[chunk, step],
            out_recv.at[chunk, step],
            rel=peer,
        )

    def own_copy(chunk):
        return pltpu.make_async_copy(
            total.at[chunk, pl.ds(pl.multiple_of(rel * group, 8), group), :],
            out.at[rel, :, pl.ds(chunk * LANES, LANES)],
            load_sem.at[5 + chunk],
        )

    def finish(chunk):
        columns = slice(chunk * LANES, (chunk + 1) * LANES)

        def close(owner_rel):
            place = pl.ds(pl.multiple_of(owner_rel * group, 8), group)
            total[chunk, place, :] = scale[place, :] * total[chunk, place, :] + bias[:, columns]

        for step, peer in ((3, far_rel), (1, x_rel), (2, y_rel)):
            close(peer)
            out_copy(chunk, step).start()
        close(rel)
        own_copy(chunk).start()

    def add_own(chunk):
        def one(t, carry):
            add_field(chunk, node, t)
            return carry

        lax.fori_loop(0, row_tiles, one, 0)

    def send_rest(first_chunk):
        for chunk in range(first_chunk, chunks):
            for t in range(row_tiles):
                send_own(chunk, t)

    pl.when(feat == 0)(lambda: send_rest(1))
    for chunk in range(chunks):
        add_own(chunk)
    pl.when(feat != 0)(lambda: send_rest(0))

    def hop_step(s, carry):
        for chunk in range(chunks):
            take(chunk, s)
        return carry

    lax.fori_loop(1, last, hop_step, 0)
    take(0, last)
    finish(0)

    def drain_raw(slot, carry):
        for way in range(2):
            mine = slot <= node if way == 0 else slot >= node

            @pl.when(both_and(onward(way), mine))
            def _(way=way):
                for t in range(row_tiles):
                    z_copy(way, slot, "O", t).wait_send()

            @pl.when(both_and(onward(way), mine, slot != node))
            def _(way=way):
                z_copy(way, slot, "F", 2).wait_send()

        @pl.when(slot != node)
        def _():
            s = jnp.abs(slot - node)
            for sends in (x_sends, y_sends):
                for condition, copy in sends(slot, s):
                    act_if(condition, lambda: copy().wait_send())

        return carry

    lax.fori_loop(0, nodes, drain_raw, 0)
    for way in range(2):

        @pl.when(onward(way))
        def _(way=way):
            for condition, copy in z_extras(way):
                act_if(condition, lambda: copy().wait_send())

    for step in range(1, nodes):
        scale_copy(node, step).wait_send()
    for t in range(row_tiles):
        pair_copy(t).wait_send()
    for chunk in range(1, chunks):
        take(chunk, last)
        finish(chunk)

    def drain_line(slot, carry):
        for way in range(2):
            mine = slot <= node if way == 0 else slot >= node

            @pl.when(both_and(onward(way), mine))
            def _(way=way):
                for chunk in range(chunks):
                    for t in range(row_tiles):
                        line_copy(chunk, way, slot, t).wait_send()

        return carry

    lax.fori_loop(0, nodes, drain_line, 0)
    for chunk in range(chunks):
        own_copy(chunk).wait()
        for step in range(1, rels):
            out_copy(chunk, step).wait_send()
            in_copy(chunk, step).wait_recv()


def on_device(
    nodes, rels, features, tile_values, tile_cols, tile_count, degree, proj_weight, proj_bias
):
    rows, depth = features.shape
    _, row_tiles, slots, tile, _ = tile_values.shape
    width = proj_bias.shape[1]
    chunks = width // LANES
    col_tiles = nodes * row_tiles
    hbm = pl.BlockSpec(memory_space=pl.ANY)
    smem = pl.BlockSpec(memory_space=pltpu.SMEM)
    dma = pltpu.SemaphoreType.DMA
    return pl.pallas_call(
        functools.partial(kernel, (nodes, rels, chunks)),
        out_shape=pltpu.VMEM((rels, rows // rels, width), jnp.float32),
        in_specs=[smem, smem] + [hbm] * 5,
        out_specs=hbm,
        scratch_shapes=[
            pltpu.SMEM((row_tiles * col_tiles,), jnp.int32),
            pltpu.VMEM((1, width), jnp.float32),
            pltpu.VMEM((1, rows), jnp.int32),
            pltpu.VMEM((depth, 2 * width), jnp.float32),
            pltpu.VMEM((rows, LANES), jnp.float32),
            pltpu.VMEM((row_tiles, slots, tile, tile), jnp.float32),
            pltpu.VMEM((row_tiles, slots + 1, tile, tile), jnp.bfloat16),
            pltpu.VMEM((row_tiles, slots + 1, tile, tile), jnp.bfloat16),
            pltpu.VMEM((2, depth, 2 * width), jnp.bfloat16),
            pltpu.VMEM((nodes, rows, depth), jnp.float32),
            pltpu.VMEM((nodes, SUBLANES, tile), jnp.float32),
            pltpu.VMEM((rows, depth), jnp.float32),
            pltpu.VMEM((chunks, nodes, rows, LANES), jnp.float32),
            pltpu.VMEM((chunks, rows, LANES), jnp.float32),
            pltpu.VMEM((row_tiles, tile, width), jnp.float32),
            pltpu.VMEM((row_tiles, tile, width), jnp.float32),
            pltpu.VMEM((2, tile, 2 * depth), jnp.bfloat16),
            dma((5 + chunks,)),
            dma((nodes,)),
            dma((nodes,)),
            dma((nodes, row_tiles, rels)),
            dma((2, nodes, 10)),
            dma((nodes, row_tiles + 1)),
            dma((nodes, row_tiles + 1)),
            dma((row_tiles,)),
            dma((row_tiles,)),
            dma((chunks, 2, nodes, row_tiles)),
            dma((chunks, nodes, row_tiles)),
            dma((chunks, rels)),
            dma((chunks, rels)),
        ],
        compiler_params=pltpu.CompilerParams(
            collective_id=0, has_side_effects=True, vmem_limit_bytes=60 << 20
        ),
    )(
        tile_cols.transpose(1, 0, 2),
        tile_count,
        degree,
        proj_weight[0],
        proj_bias,
        features,
        tile_values[0],
    )


def solution(mesh):
    return jax.shard_map(
        functools.partial(on_device, mesh.shape["node"], mesh.shape["rel"]),
        mesh=mesh,
        in_specs=(
            P("node", "feat"),
            P("rel", "node", None, None, None),
            P("rel", "node", None),
            P("rel", "node"),
            P("rel", "node"),
            P("rel", "feat", None),
            P("rel", "feat"),
        ),
        out_specs=P(None, ("node", "rel"), "feat"),
        check_vma=False,
    )
```
